32 devices in a mesh: blk: 16 (over z, x, core), mp: 2 (over y).
Axes of the slice: x: 2, y: 2, z: 4, core: 2. Of those that a mesh axis runs over, the one named last changes fastest.
Arguments:
- anchors: bfloat16 [8192, 1024], P('blk', 'mp'), may hold values from -0.5833631 to 0.5833631, as said below
- partners: bfloat16 [8192, 1024], P('blk', 'mp'), may hold values from -0.5833631 to 0.5833631, as said below
- row_lse: float32 [8192], P('blk'), as said below
- anchor_acc: float32 [8192, 1024], P('blk', 'mp'), may hold values from -6 to 6
- partner_acc: float32 [8192, 1024], P('blk', 'mp'), may hold values from -6 to 6
- match_dev: int32 [8192], P('blk'), may hold values from 0 to 15, as said below
- match_row: int32 [8192], P('blk'), may hold values from 0 to 511
Outputs:
- anchor_grad: float32 [8192, 1024], P('blk', 'mp')
- partner_out: float32 [8192, 1024], P('blk', 'mp')
The draws below stay inside these ranges and needn't reach their ends.
Inputs may be any that keep to these rules, and one draw needn't show every extreme that they name: Within each block of 512 rows every block index appears exactly 32 times, and the pairs (match_dev, match_row) name every partner row exactly once. `anchors`: entries are independent with mean 0 and standard deviation 0.55 / 1024 ** 0.25. `partners`: entries are independent with mean 0 and standard deviation 0.55 / 1024 ** 0.25. `row_lse`: each entry lies within 1.5 of log(1024) + 4.5.
All inputs are finite; a program needn't handle non-finite values.
Results may differ from the reference program's by a relative error of at most 0.0085.
Values may be sent and summed in bfloat16 or wider, within the bound.
No kernel may reach another device: no remote copies, remote signals or barrier semaphores. Data moves between devices by JAX's collectives and lax.ppermute only.
A program may use at most 64 MiB of HBM per device.

```python
import math
import jax
import jax.numpy as jnp
from jax import lax

D = 1024
R = 512
ROWS = 8192
N_BLK = 16


def matching(key):
    key = jax.random.fold_in(key, 7)
    anchor_key, partner_key = jax.random.split(key)
    per_peer = R // N_BLK
    anchor_perm = jax.vmap(lambda subkey: jax.random.permutation(subkey, R))(jax.random.split(anchor_key, N_BLK))
    partner_perm = jax.vmap(lambda subkey: jax.random.permutation(subkey, R))(jax.random.split(partner_key, N_BLK))
    slot_ids = jnp.arange(R, dtype=jnp.int32)
    block_ids = jnp.arange(N_BLK, dtype=jnp.int32)[:, None]
    dev_slot = jnp.broadcast_to(slot_ids // per_peer, (N_BLK, R))
    row_slot = partner_perm[dev_slot, block_ids * per_peer + slot_ids[None, :] % per_peer]
    inverse = jnp.argsort(anchor_perm, axis=1)
    match_devs = jnp.take_along_axis(dev_slot, inverse, axis=1).reshape(-1)
    match_rows = jnp.take_along_axis(row_slot, inverse, axis=1).reshape(-1)
    return (match_devs.astype(jnp.int32), match_rows.astype(jnp.int32))


def draw_match_dev(key, part):
    return matching(key)[0]


def draw_match_row(key, part):
    return matching(key)[1]


def draw_anchors(key, part):
    key = jax.random.fold_in(key, 11)
    spread = 0.55 / D ** 0.25
    values = jnp.clip(jax.random.normal(key, (ROWS, D), jnp.float32) * spread, -6.0 * spread, 6.0 * spread)
    return values.astype(jnp.bfloat16)


def draw_partners(key, part):
    key = jax.random.fold_in(key, 13)
    spread = 0.55 / D ** 0.25
    values = jnp.clip(jax.random.normal(key, (ROWS, D), jnp.float32) * spread, -6.0 * spread, 6.0 * spread)
    return values.astype(jnp.bfloat16)


def draw_row_lse(key, part):
    key = jax.random.fold_in(key, 17)
    center = math.log(2.0 * R) + 4.5
    offset = jax.random.uniform(key, (ROWS,), jnp.float32, -1.5, 1.5)
    return (center + offset).astype(jnp.float32)


def level_of(key, extent, shards, least, largest):
    def one(position, shards_of):
        heights = jax.random.uniform(jax.random.fold_in(jax.random.fold_in(key, 6), position), (shards_of,), jnp.float32, least / len(shards), largest / len(shards))
        return jnp.repeat(jnp.exp(heights), extent[position] // shards_of).reshape((-1,) + (1,) * (len(extent) - position - 1))

    loudness = one(*shards[0])
    for cut in shards[1:]:
        loudness = loudness * one(*cut)
    return loudness


def gaussian(own_key, shape, deviation, limit, cuts=(), kind=jnp.bfloat16):
    entries = deviation * jax.random.normal(own_key, shape, jnp.float32)
    if cuts:
        entries = entries * level_of(own_key, shape, cuts, -0.22, 0.18)
    return jnp.clip(entries, -limit, limit).astype(kind)


def setup_inputs(seed: int = 0) -> dict:
    key_of = jax.random.split(jax.random.key(seed), 8)
    anchors = draw_anchors(jax.random.fold_in(key_of[7], 71), 0)
    partners = draw_partners(jax.random.fold_in(key_of[7], 71), 0)
    row_lse = draw_row_lse(jax.random.fold_in(key_of[7], 71), 0)
    anchor_acc = gaussian(key_of[3], (ROWS, D), 1.0, 6.0, ((0, 16), (1, 2)), jnp.float32)
    partner_acc = gaussian(key_of[4], (ROWS, D), 1.0, 6.0, ((0, 16), (1, 2)), jnp.float32)
    match_dev = draw_match_dev(jax.random.fold_in(key_of[7], 71), 0)
    match_row = draw_match_row(jax.random.fold_in(key_of[7], 71), 0)
    return {"anchors": anchors, "partners": partners, "row_lse": row_lse, "anchor_acc": anchor_acc, "partner_acc": partner_acc, "match_dev": match_dev, "match_row": match_row}


SCALE = 10.0


def contract_rows(left, right):
    return lax.dot_general(left, right, (((1,), (1,)), ((), ())), preferred_element_type=jnp.float32)


def contract_cols(left, right):
    return lax.dot_general(left, right, (((0,), (0,)), ((), ())), preferred_element_type=jnp.float32)


def tile_terms(inputs):
    anchor_block, own_block, prior_block, lse_block = inputs
    weight_own = jnp.exp(SCALE * contract_rows(anchor_block, own_block) - lse_block[:, None]).astype(jnp.bfloat16)
    weight_prior = jnp.exp(SCALE * contract_rows(anchor_block, prior_block) - lse_block[:, None]).astype(jnp.bfloat16)
    toward = SCALE * (jnp.dot(weight_own, own_block, preferred_element_type=jnp.float32)
                      + jnp.dot(weight_prior, prior_block, preferred_element_type=jnp.float32))
    own_terms = SCALE * contract_cols(weight_own, anchor_block)
    prior_terms = SCALE * contract_cols(weight_prior, anchor_block)
    return toward, own_terms, prior_terms


def reference(anchors, partners, row_lse, anchor_acc, partner_acc, match_dev, match_row):
    anchor_blocks = anchors.reshape(N_BLK, R, D)
    partner_blocks = partners.reshape(N_BLK, R, D)
    prior_blocks = jnp.roll(partner_blocks, 1, axis=0)
    toward, own_terms, prior_terms = lax.map(
        tile_terms, (anchor_blocks, partner_blocks, prior_blocks, row_lse.reshape(N_BLK, R)))
    flat_index = (match_dev * R + match_row).astype(jnp.int32)
    positive = jnp.take(partners, flat_index, axis=0)
    anchor_grad = anchor_acc + toward.reshape(N_BLK * R, D) - SCALE * positive.astype(jnp.float32)
    home = jnp.zeros((N_BLK * R, D), jnp.float32).at[flat_index].set(-SCALE * anchors.astype(jnp.float32))
    before = (partner_acc + home).reshape(N_BLK, R, D) + own_terms
    partner_out = jnp.roll(before, 1, axis=0) + prior_terms
    return anchor_grad, partner_out.reshape(N_BLK * R, D)
```

```python
import functools
import jax
import jax.numpy as jnp
from jax import lax
from jax.experimental import pallas as pl
from jax.experimental.pallas import tpu as pltpu
from jax.sharding import PartitionSpec as P

SCALE = 10.0
LANES = 128
BF16 = jnp.bfloat16
F32 = jnp.float32
I32 = jnp.int32


def shifted(value, axis, steps):
    count = lax.axis_size(axis)
    pairs = [(source, (source + steps) % count) for source in range(count)]
    return lax.ppermute(value, axis, pairs)


def dot_nt(left, right):
    return lax.dot_general(left, right, (((1,), (1,)), ((), ())), preferred_element_type=F32)


def dot_nn(left, right):
    return lax.dot_general(left, right, (((1,), (0,)), ((), ())), preferred_element_type=F32)


def dot_tn(left, right):
    return lax.dot_general(left, right, (((0,), (0,)), ((), ())), preferred_element_type=F32)


def iota(shape, dimension):
    return lax.broadcasted_iota(I32, shape, dimension)


def one_hot(condition):
    return jnp.where(condition, 1.0, 0.0).astype(BF16)


def split_digits(values):
    return (values >> 8).astype(F32), (values & 255).astype(F32)


def rank_kernel(blocks, per_peer, dev_ref, row_ref, want_ref, slot_ref):
    rows = dev_ref.shape[1]
    dev = dev_ref[...]
    chosen = iota((blocks, rows), 0) == dev
    member = one_hot(chosen)
    earlier = one_hot(iota((rows, rows), 0) < iota((rows, rows), 1))
    before = dot_nn(member, earlier)
    rank = jnp.sum(jnp.where(chosen, before, 0.0), axis=0, keepdims=True).astype(I32)
    slot_ref[...] = dev * per_peer + rank
    place = one_hot(iota((LANES, rows), 0) == rank)
    high, low = split_digits(row_ref[...])
    wanted = 256.0 * dot_nt(jnp.where(chosen, high, 0.0).astype(BF16), place)
    wanted = wanted + dot_nt(jnp.where(chosen, low, 0.0).astype(BF16), place)
    wanted = wanted.astype(I32)
    want_ref[:, 0, :] = wanted
    want_ref[1:, 1, :] = wanted[:-1]
    want_ref[:1, 1, :] = wanted[-1:]


def listed(blocks, per_peer, table, along_lanes):
    count = blocks * per_peer
    high, low = split_digits(table)
    high, low = high.astype(BF16), low.astype(BF16)
    if along_lanes:
        spread = one_hot(iota((LANES, count), 0) == iota((LANES, count), 1) % per_peer)
        values = 256.0 * dot_nn(high, spread) + dot_nn(low, spread)
        mine = iota((blocks, count), 0) == iota((blocks, count), 1) // per_peer
        return jnp.sum(jnp.where(mine, values, 0.0), axis=0, keepdims=True).astype(I32)
    spread = one_hot(iota((count, LANES), 1) == iota((count, LANES), 0) % per_peer)
    values = 256.0 * dot_nt(spread, high) + dot_nt(spread, low)
    mine = iota((count, blocks), 1) == iota((count, blocks), 0) // per_peer
    return jnp.sum(jnp.where(mine, values, 0.0), axis=1, keepdims=True).astype(I32)


def serve_kernel(blocks, per_peer, asked_ref, slot_ref, anchors_ref, partners_ref, send_ref):
    rows = anchors_ref.shape[0]
    asked = listed(blocks, per_peer, asked_ref[:, 0, :], False)
    found = dot_nn(one_hot(asked == iota((rows, rows), 1)), partners_ref[...]).astype(BF16)
    slot = slot_ref[...] + per_peer
    slot = jnp.where(slot >= rows, slot - rows, slot)
    ordered = dot_nn(one_hot(iota((rows, rows), 0) == slot), anchors_ref[...]).astype(BF16)
    for block in range(blocks):
        part = slice(block * per_peer, (block + 1) * per_peer)
        send_ref[block, :per_peer, :] = found[part]
        send_ref[block, per_peer:, :] = ordered[part]


def as_column(row):
    count = row.shape[1]
    diagonal = iota((count, count), 0) == iota((count, count), 1)
    return jnp.sum(jnp.where(diagonal, row, 0.0), axis=1, keepdims=True)


def own_kernel(
    anchors_ref, other_anchors_ref, partners_ref, other_partners_ref, lse_ref, anchor_acc_ref, partner_acc_ref,
    toward_ref, staying_ref,
):
    logits = dot_nt(anchors_ref[...], partners_ref[...]) + dot_nt(other_anchors_ref[...], other_partners_ref[...])
    weights = jnp.exp(SCALE * logits - as_column(lse_ref[...])).astype(BF16)
    staying = partner_acc_ref[...] + SCALE * dot_tn(weights, anchors_ref[...])
    staying_ref[...] = staying.astype(BF16)
    toward_ref[...] = anchor_acc_ref[...] + SCALE * dot_nn(weights, partners_ref[...])


def prior_kernel(
    anchors_ref, other_anchors_ref, previous_ref, other_even_ref, other_odd_ref, lse_ref, toward_ref,
    anchor_ref, partner_ref,
):
    other_previous = other_even_ref[...] + other_odd_ref[...]
    logits = dot_nt(anchors_ref[...], previous_ref[...]) + dot_nt(other_anchors_ref[...], other_previous)
    weights = jnp.exp(SCALE * logits - as_column(lse_ref[...])).astype(BF16)
    anchor_ref[...] = toward_ref[...] + SCALE * dot_nn(weights, previous_ref[...])
    partner_ref[...] = SCALE * dot_tn(weights, anchors_ref[...])


def final_kernel(
    blocks, per_peer, got_ref, asked_ref, slot_ref, anchor_ref, partner_ref, arrived_ref,
    anchor_out_ref, partner_out_ref,
):
    rows = anchor_ref.shape[0]
    width = anchor_ref.shape[1]
    fetched = jnp.concatenate([got_ref[block, :per_peer, :] for block in range(blocks)], axis=0)
    home = jnp.concatenate([got_ref[block, per_peer:, :] for block in range(blocks)], axis=0)
    pick = one_hot(iota((rows, rows), 0) == slot_ref[...])
    anchor_out_ref[...] = anchor_ref[...] - SCALE * dot_tn(pick, fetched)
    asked = listed(blocks, per_peer, asked_ref[:, 1, :], True)
    put = one_hot(iota((rows, rows), 0) == asked)
    partner_out_ref[...] = arrived_ref[...].astype(F32) + partner_ref[...] - SCALE * dot_nn(put, home)


def call(kernel, name, flops, outs, *operands):
    size = sum(value.size * value.dtype.itemsize for value in (*operands, *outs))
    return pl.pallas_call(
        kernel,
        out_shape=outs,
        name=name,
        cost_estimate=pl.CostEstimate(flops=flops, bytes_accessed=size, transcendentals=0),
        compiler_params=pltpu.CompilerParams(vmem_limit_bytes=40 * 1024 * 1024),
    )(*operands)


def on_device(anchors, partners, row_lse, anchor_acc, partner_acc, match_dev, match_row):
    rows, width = anchors.shape
    blocks = lax.axis_size("blk")
    per_peer = rows // blocks
    shape = jax.ShapeDtypeStruct
    cube = 2 * rows * rows * width

    want, slot = call(
        functools.partial(rank_kernel, blocks, per_peer), "rank", cube // 8,
        (shape((blocks, 2, LANES), I32), shape((1, rows), I32)),
        match_dev.reshape(1, rows), match_row.reshape(1, rows),
    )
    other_anchors = shifted(anchors, "mp", 1)
    other_partners = shifted(partners, "mp", 1)
    previous = shifted(partners, "blk", 1)
    asked = lax.all_to_all(want, "blk", split_axis=0, concat_axis=0, tiled=True)

    asked, previous, other_partners = lax.optimization_barrier((asked, previous, other_partners))

    across = [(2 * block + half, 2 * block + 1 - half) for block in range(0, blocks, 2) for half in range(2)]
    other_even = lax.ppermute(previous, ("blk", "mp"), across)
    other_odd = lax.ppermute(other_partners, "blk", [(block, block + 1) for block in range(0, blocks, 2)])

    (send,) = call(
        functools.partial(serve_kernel, blocks, per_peer), "serve", 2 * cube,
        (shape((blocks, 2 * per_peer, width), BF16),),
        asked, slot, anchors, partners,
    )
    got = lax.all_to_all(send, "blk", split_axis=0, concat_axis=0, tiled=True)

    lse_row = row_lse.reshape(1, rows)
    toward, staying = call(
        own_kernel, "own", 4 * cube,
        (shape((rows, width), F32), shape((rows, width), BF16)),
        anchors, other_anchors, partners, other_partners, lse_row, anchor_acc, partner_acc,
    )
    arrived = shifted(staying, "blk", 1)
    anchor_part, partner_part = call(
        prior_kernel, "prior", 4 * cube,
        (shape((rows, width), F32), shape((rows, width), F32)),
        anchors, other_anchors, previous, other_even, other_odd, lse_row, toward,
    )
    return call(
        functools.partial(final_kernel, blocks, per_peer), "final", 2 * cube,
        (shape((rows, width), F32), shape((rows, width), F32)),
        got, asked, slot, anchor_part, partner_part, arrived,
    )


def solution(mesh):
    return jax.shard_map(
        on_device,
        mesh=mesh,
        in_specs=(
            P("blk", "mp"),
            P("blk", "mp"),
            P("blk"),
            P("blk", "mp"),
            P("blk", "mp"),
            P("blk"),
            P("blk"),
        ),
        out_specs=(P("blk", "mp"), P("blk", "mp")),
        check_vma=False,
    )
```

```python
import functools
import jax
import jax.numpy as jnp
from jax import lax
from jax.experimental import pallas as pl
from jax.experimental.pallas import tpu as pltpu
from jax.sharding import PartitionSpec as P

SCALE = 10.0
LANES = 128
EXTRA = 16
COST = dict(rank=1, serve=0, own=16, prior=16, final=8)
MID = 40_000_000
SERVE = 63_400_000
BF16 = jnp.bfloat16
F32 = jnp.float32
I32 = jnp.int32


def shifted(value, axis, steps):
    count = lax.axis_size(axis)
    pairs = [(source, (source + steps) % count) for source in range(count)]
    return lax.ppermute(value, axis, pairs)


def dot_nt(left, right):
    return lax.dot_general(left, right, (((1,), (1,)), ((), ())), preferred_element_type=F32)


def dot_nn(left, right):
    return lax.dot_general(left, right, (((1,), (0,)), ((), ())), preferred_element_type=F32)


def dot_tn(left, right):
    return lax.dot_general(left, right, (((0,), (0,)), ((), ())), preferred_element_type=F32)


def iota(shape, dimension):
    return lax.broadcasted_iota(I32, shape, dimension)


def one_hot(condition):
    return jnp.where(condition, 1.0, 0.0).astype(BF16)


def split_digits(values):
    return (values >> 8).astype(F32), (values & 255).astype(F32)


def begin(*pairs):
    copies = [pltpu.make_async_copy(*pair) for pair in pairs]
    for copy in copies:
        copy.start()
    return copies


def rank_kernel(
    blocks, per_peer, padded, dev_hbm, row_hbm, anchors_hbm, send_hbm, slot_ref,
    dev_ref, row_ref, anchors_ref, ordered_ref, digits_ref, packed_ref, sems,
):
    copies = begin(
        (dev_hbm, dev_ref, sems.at[0]), (row_hbm, row_ref, sems.at[1]), (anchors_hbm, anchors_ref, sems.at[2])
    )
    rows, width = anchors_ref.shape
    earlier = one_hot(iota((rows, rows), 0) < iota((rows, rows), 1))
    digits_ref[...] = jnp.zeros_like(digits_ref)
    copies[0].wait()
    dev = dev_ref[...].reshape(1, rows)
    chosen = iota((blocks, rows), 0) == dev
    before = dot_nn(one_hot(chosen), earlier)
    rank = jnp.sum(jnp.where(chosen, before, 0.0), axis=0, keepdims=True).astype(I32)
    slot_ref[...] = dev * per_peer + rank
    after = jnp.where(dev == blocks - 1, 0, dev + 1)
    pick = one_hot(iota((blocks * padded, rows), 0) == after * padded + rank)
    copies[2].wait()
    ordered = dot_nn(pick, anchors_ref[...]).astype(BF16)
    ordered_ref[...] = ordered.reshape(ordered_ref.shape)
    outgoing = begin(*[
        (
            ordered_ref.at[:, :, pl.ds(part * LANES, LANES)],
            send_hbm.at[:, pl.ds(part * padded, padded), :],
            sems.at[3 + part],
        )
        for part in range(width // LANES)
    ])
    place = one_hot(iota((LANES, rows), 0) == rank)
    copies[1].wait()
    for digit, values in enumerate(split_digits(row_ref[...].reshape(1, rows))):
        wanted = dot_nt(jnp.where(chosen, values, 0.0).astype(BF16), place)
        digits_ref[:, digit, :] = wanted
        digits_ref[1:, 2 + digit, :] = wanted[:-1]
        digits_ref[:1, 2 + digit, :] = wanted[-1:]
    packed_ref[...] = digits_ref[...].astype(BF16)
    outgoing += begin((packed_ref, send_hbm.at[:, pl.ds(width // LANES * padded, EXTRA), :], sems.at[3 + width // LANES]))
    for copy in outgoing:
        copy.wait()


def listed_column(blocks, per_peer, high, low):
    count = blocks * per_peer
    spread = one_hot(iota((count, LANES), 1) == iota((count, LANES), 0) % per_peer)
    values = 256.0 * dot_nt(spread, high) + dot_nt(spread, low)
    mine = iota((count, blocks), 1) == iota((count, blocks), 0) // per_peer
    return jnp.sum(jnp.where(mine, values, 0.0), axis=1, keepdims=True).astype(I32)


def listed_row(blocks, per_peer, padded, high, low):
    count = blocks * padded
    place = iota((LANES, count), 1) % padded
    spread = one_hot(iota((LANES, count), 0) == place)
    values = 256.0 * dot_nn(high, spread) + dot_nn(low, spread)
    mine = iota((blocks, count), 0) == iota((blocks, count), 1) // padded
    asked = jnp.sum(jnp.where(mine, values, 0.0), axis=0, keepdims=True).astype(I32)
    return jnp.where(iota((1, count), 1) % padded < per_peer, asked, -1)


def serve_kernel(blocks, per_peer, got_hbm, partners_hbm, send_ref, packed_ref, partners_ref, sems):
    rows, width = partners_ref.shape
    table, fetch = begin(
        (got_hbm.at[:, pl.ds(got_hbm.shape[1] - EXTRA, EXTRA), :], packed_ref, sems.at[0]),
        (partners_hbm, partners_ref, sems.at[1]),
    )
    table.wait()
    digits = packed_ref[...].astype(F32)
    asked = listed_column(blocks, per_peer, digits[:, 0, :].astype(BF16), digits[:, 1, :].astype(BF16))
    pick = one_hot(asked == iota((rows, rows), 1))
    fetch.wait()
    send_ref[...] = dot_nn(pick, partners_ref[...]).astype(BF16)


def as_column(row):
    count = row.shape[1]
    diagonal = iota((count, count), 0) == iota((count, count), 1)
    return jnp.sum(jnp.where(diagonal, row, 0.0), axis=1, keepdims=True)


def own_kernel(
    anchors_ref, other_anchors_ref, partners_ref, other_partners_ref, lse_ref, anchor_acc_ref, partner_acc_ref,
    toward_ref, staying_ref,
):
    logits = dot_nt(anchors_ref[...], partners_ref[...]) + dot_nt(other_anchors_ref[...], other_partners_ref[...])
    weights = jnp.exp(SCALE * logits - as_column(lse_ref[...])).astype(BF16)
    staying = partner_acc_ref[...] + SCALE * dot_tn(weights, anchors_ref[...])
    staying_ref[...] = staying.astype(BF16)
    toward_ref[...] = anchor_acc_ref[...] + SCALE * dot_nn(weights, partners_ref[...])


def prior_kernel(
    blocks, per_peer, padded,
    anchors_ref, other_anchors_ref, previous_ref, other_even_ref, other_odd_ref, lse_ref, toward_ref, got_hbm,
    anchor_ref, partner_ref, home_ref, packed_ref, sems,
):
    rows, width = anchors_ref.shape
    copies = begin(
        (got_hbm.at[:, pl.ds(width // LANES * padded, EXTRA), :], packed_ref, sems.at[0]),
        *[
            (
                got_hbm.at[:, pl.ds(part * padded, padded), :],
                home_ref.at[:, :, pl.ds(part * LANES, LANES)],
                sems.at[1 + part],
            )
            for part in range(width // LANES)
        ],
    )
    other_previous = other_even_ref[...] + other_odd_ref[...]
    logits = dot_nt(anchors_ref[...], previous_ref[...]) + dot_nt(other_anchors_ref[...], other_previous)
    weights = jnp.exp(SCALE * logits - as_column(lse_ref[...])).astype(BF16)
    anchor_ref[...] = toward_ref[...] + SCALE * dot_nn(weights, previous_ref[...])
    for copy in copies:
        copy.wait()
    digits = packed_ref[...].astype(F32)
    asked = listed_row(blocks, per_peer, padded, digits[:, 2, :].astype(BF16), digits[:, 3, :].astype(BF16))
    put = one_hot(iota((rows, blocks * padded), 0) == asked)
    home = dot_nn(put, home_ref[...].reshape(blocks * padded, width))
    partner_ref[...] = SCALE * dot_tn(weights, anchors_ref[...]) - SCALE * home


def final_kernel(fetched_hbm, slot_hbm, anchor_hbm, out_ref, fetched_ref, slot_ref, anchor_ref, sems):
    rows, width = anchor_ref.shape
    copies = begin(
        (slot_hbm, slot_ref, sems.at[0]), (fetched_hbm, fetched_ref, sems.at[1]), (anchor_hbm, anchor_ref, sems.at[2])
    )
    copies[0].wait()
    slot = as_column(slot_ref[...].astype(F32)).astype(I32)
    pick = one_hot(iota((rows, rows), 1) == slot)
    copies[1].wait()
    copies[2].wait()
    out_ref[...] = anchor_ref[...] - SCALE * dot_nn(pick, fetched_ref[...])


def call(kernel, name, flops, outs, operands, spaces=None, out_space=None, scratch=(), aliases=None, limit=63_400_000):
    size = sum(value.size * value.dtype.itemsize for value in (*operands, *outs))
    spaces = spaces or "v" * len(operands)
    specs = [pl.BlockSpec(memory_space={"v": pltpu.VMEM, "h": pltpu.HBM}[space]) for space in spaces]
    return pl.pallas_call(
        kernel,
        out_shape=outs,
        name=name,
        in_specs=specs,
        out_specs=tuple(pl.BlockSpec(memory_space=space) for space in out_space or (pltpu.VMEM,) * len(outs)),
        scratch_shapes=list(scratch),
        input_output_aliases=aliases or {},
        cost_estimate=pl.CostEstimate(flops=flops, bytes_accessed=size, transcendentals=0),
        compiler_params=pltpu.CompilerParams(vmem_limit_bytes=limit),
    )(*operands)


def on_device(anchors, partners, row_lse, anchor_acc, partner_acc, match_dev, match_row):
    rows, width = anchors.shape
    blocks = lax.axis_size("blk")
    per_peer = rows // blocks
    shape = jax.ShapeDtypeStruct
    dma = pltpu.SemaphoreType.DMA
    cube = 2 * rows * rows * width

    assert per_peer <= LANES and width % LANES == 0
    padded = -(-per_peer // 16) * 16
    tall = width // LANES * padded + EXTRA

    send, slot = call(
        functools.partial(rank_kernel, blocks, per_peer, padded), "rank", COST["rank"] * cube // 4,
        (shape((blocks, tall, LANES), BF16), shape((1, rows), I32)),
        (match_dev, match_row, anchors), spaces="hhh", out_space=(pltpu.HBM, pltpu.VMEM),
        scratch=(
            pltpu.VMEM((rows,), I32), pltpu.VMEM((rows,), I32), pltpu.VMEM((rows, width), BF16),
            pltpu.VMEM((blocks, padded, width), BF16), pltpu.VMEM((blocks, EXTRA, LANES), F32),
            pltpu.VMEM((blocks, EXTRA, LANES), BF16), dma((4 + width // LANES,)),
        ),
    )
    got = lax.all_to_all(send, "blk", split_axis=0, concat_axis=0, tiled=True)

    other_anchors = shifted(anchors, "mp", 1)
    other_partners = shifted(partners, "mp", 1)
    got, ring_partners = lax.optimization_barrier((got, partners))
    previous = shifted(ring_partners, "blk", 1)
    got, other_anchors = lax.optimization_barrier((got, other_anchors))
    across = [(2 * block + half, 2 * block + 1 - half) for block in range(0, blocks, 2) for half in range(2)]
    other_even = lax.ppermute(previous, ("blk", "mp"), across)
    other_odd = lax.ppermute(other_partners, "blk", [(block, block + 1) for block in range(0, blocks, 2)])

    (found,) = call(
        functools.partial(serve_kernel, blocks, per_peer), "serve", COST["serve"] * cube // 4,
        (shape((rows, width), BF16),),
        (got, partners), spaces="hh", limit=SERVE,
        scratch=(pltpu.VMEM((blocks, EXTRA, LANES), BF16), pltpu.VMEM((rows, width), BF16), dma((2,))),
    )
    fetched = lax.all_to_all(
        found.reshape(blocks, per_peer, width), "blk", split_axis=0, concat_axis=0, tiled=True
    ).reshape(rows, width)

    lse_row = row_lse.reshape(1, rows)
    toward, staying = call(
        own_kernel, "own", COST["own"] * cube // 4,
        (shape((rows, width), F32), shape((rows, width), BF16)),
        (anchors, other_anchors, partners, other_partners, lse_row, anchor_acc, partner_acc), limit=MID,
    )
    arrived = shifted(staying, "blk", 1)
    anchor_part, partner_part = call(
        functools.partial(prior_kernel, blocks, per_peer, padded), "prior", COST["prior"] * cube // 4,
        (shape((rows, width), F32), shape((rows, width), F32)),
        (anchors, other_anchors, previous, other_even, other_odd, lse_row, toward, got), spaces="vvvvvvvh", limit=MID,
        scratch=(
            pltpu.VMEM((blocks, padded, width), BF16), pltpu.VMEM((blocks, EXTRA, LANES), BF16),
            dma((1 + width // LANES,)),
        ),
    )
    partner_out = arrived.astype(F32) + partner_part
    (anchor_grad,) = call(
        final_kernel, "final", COST["final"] * cube // 4,
        (shape((rows, width), F32),),
        (fetched, slot, anchor_part), spaces="hhh",
        scratch=(
            pltpu.VMEM((rows, width), BF16), pltpu.VMEM(slot.shape, I32), pltpu.VMEM((rows, width), F32), dma((3,)),
        ),
    )
    return anchor_grad, partner_out


def solution(mesh):
    return jax.shard_map(
        on_device,
        mesh=mesh,
        in_specs=(
            P("blk", "mp"),
            P("blk", "mp"),
            P("blk"),
            P("blk", "mp"),
            P("blk", "mp"),
            P("blk"),
            P("blk"),
        ),
        out_specs=(P("blk", "mp"), P("blk", "mp")),
        check_vma=False,
    )
```

```python
import functools
import jax
import jax.numpy as jnp
from jax import lax
from jax.experimental import pallas as pl
from jax.experimental.pallas import tpu as pltpu
from jax.sharding import PartitionSpec as P

SCALE = 10.0
LANES = 128
EXTRA = 8
COST = dict(rank=1, serve=0, own=16, prior=16, final=8)
MID = 40_000_000
SERVE = 63_400_000
BF16 = jnp.bfloat16
F32 = jnp.float32
I32 = jnp.int32


def shifted(value, axis, steps):
    count = lax.axis_size(axis)
    pairs = [(source, (source + steps) % count) for source in range(count)]
    return lax.ppermute(value, axis, pairs)


def dot_nt(left, right):
    return lax.dot_general(left, right, (((1,), (1,)), ((), ())), preferred_element_type=F32)


def dot_nn(left, right):
    return lax.dot_general(left, right, (((1,), (0,)), ((), ())), preferred_element_type=F32)


def dot_tn(left, right):
    return lax.dot_general(left, right, (((0,), (0,)), ((), ())), preferred_element_type=F32)


def iota(shape, dimension):
    return lax.broadcasted_iota(I32, shape, dimension)


def one_hot(condition):
    return jnp.where(condition, 1.0, 0.0).astype(BF16)


def split_digits(values):
    return (values >> 8).astype(F32), (values & 255).astype(F32)


def begin(*pairs):
    copies = [pltpu.make_async_copy(*pair) for pair in pairs]
    for copy in copies:
        copy.start()
    return copies


def rank_kernel(
    blocks, per_peer, padded, dev_hbm, row_hbm, anchors_hbm, send_hbm, slot_ref,
    dev_ref, row_ref, anchors_ref, ordered_ref, digits_ref, packed_ref, sems,
):
    copies = begin(
        (dev_hbm, dev_ref, sems.at[0]), (row_hbm, row_ref, sems.at[1]), (anchors_hbm, anchors_ref, sems.at[2])
    )
    rows, width = anchors_ref.shape
    earlier = one_hot(iota((rows, rows), 0) < iota((rows, rows), 1))
    digits_ref[...] = jnp.zeros_like(digits_ref)
    copies[0].wait()
    dev = dev_ref[...].reshape(1, rows)
    chosen = iota((blocks, rows), 0) == dev
    before = dot_nn(one_hot(chosen), earlier)
    rank = jnp.sum(jnp.where(chosen, before, 0.0), axis=0, keepdims=True).astype(I32)
    slot_ref[...] = dev * per_peer + rank
    after = jnp.where(dev == blocks - 1, 0, dev + 1)
    pick = one_hot(iota((blocks * padded, rows), 0) == after * padded + rank)
    copies[2].wait()
    ordered = dot_nn(pick, anchors_ref[...]).astype(BF16)
    ordered_ref[...] = ordered.reshape(ordered_ref.shape)
    outgoing = begin(*[
        (
            ordered_ref.at[:, :, pl.ds(part * LANES, LANES)],
            send_hbm.at[:, pl.ds(part * padded, padded), :],
            sems.at[3 + part],
        )
        for part in range(width // LANES)
    ])
    place = one_hot(iota((LANES, rows), 0) == rank)
    copies[1].wait()
    for digit, values in enumerate(split_digits(row_ref[...].reshape(1, rows))):
        wanted = dot_nt(jnp.where(chosen, values, 0.0).astype(BF16), place)
        digits_ref[:, digit, :] = wanted
        digits_ref[1:, 2 + digit, :] = wanted[:-1]
        digits_ref[:1, 2 + digit, :] = wanted[-1:]
    packed_ref[...] = digits_ref[...].astype(BF16)
    outgoing += begin((packed_ref, send_hbm.at[:, pl.ds(width // LANES * padded, EXTRA), :], sems.at[3 + width // LANES]))
    for copy in outgoing:
        copy.wait()


def listed_column(blocks, per_peer, high, low):
    count = blocks * per_peer
    spread = one_hot(iota((count, LANES), 1) == iota((count, LANES), 0) % per_peer)
    values = 256.0 * dot_nt(spread, high) + dot_nt(spread, low)
    mine = iota((count, blocks), 1) == iota((count, blocks), 0) // per_peer
    return jnp.sum(jnp.where(mine, values, 0.0), axis=1, keepdims=True).astype(I32)


def listed_row(blocks, per_peer, padded, high, low):
    count = blocks * padded
    place = iota((LANES, count), 1) % padded
    spread = one_hot(iota((LANES, count), 0) == place)
    values = 256.0 * dot_nn(high, spread) + dot_nn(low, spread)
    mine = iota((blocks, count), 0) == iota((blocks, count), 1) // padded
    asked = jnp.sum(jnp.where(mine, values, 0.0), axis=0, keepdims=True).astype(I32)
    return jnp.where(iota((1, count), 1) % padded < per_peer, asked, -1)


def serve_kernel(blocks, per_peer, got_hbm, partners_hbm, send_ref, packed_ref, partners_ref, sems):
    rows, width = partners_ref.shape
    table, fetch = begin(
        (got_hbm.at[:, pl.ds(got_hbm.shape[1] - EXTRA, EXTRA), :], packed_ref, sems.at[0]),
        (partners_hbm, partners_ref, sems.at[1]),
    )
    table.wait()
    digits = packed_ref[...].astype(F32)
    asked = listed_column(blocks, per_peer, digits[:, 0, :].astype(BF16), digits[:, 1, :].astype(BF16))
    pick = one_hot(asked == iota((rows, rows), 1))
    fetch.wait()
    send_ref[...] = dot_nn(pick, partners_ref[...]).astype(BF16)


def as_column(row):
    count = row.shape[1]
    diagonal = iota((count, count), 0) == iota((count, count), 1)
    return jnp.sum(jnp.where(diagonal, row, 0.0), axis=1, keepdims=True)


def own_kernel(
    anchors_ref, other_anchors_ref, partners_ref, other_partners_ref, lse_ref, anchor_acc_ref, partner_acc_ref,
    toward_ref, staying_ref,
):
    logits = dot_nt(anchors_ref[...], partners_ref[...]) + dot_nt(other_anchors_ref[...], other_partners_ref[...])
    weights = jnp.exp(SCALE * logits - as_column(lse_ref[...])).astype(BF16)
    staying = partner_acc_ref[...] + SCALE * dot_tn(weights, anchors_ref[...])
    staying_ref[...] = staying.astype(BF16)
    toward_ref[...] = anchor_acc_ref[...] + SCALE * dot_nn(weights, partners_ref[...])


def prior_kernel(
    blocks, per_peer, padded,
    anchors_ref, other_anchors_ref, previous_ref, other_even_ref, other_odd_ref, lse_ref, toward_ref, got_hbm,
    anchor_ref, partner_ref, home_ref, packed_ref, sems,
):
    rows, width = anchors_ref.shape
    copies = begin(
        (got_hbm.at[:, pl.ds(width // LANES * padded, EXTRA), :], packed_ref, sems.at[0]),
        *[
            (
                got_hbm.at[:, pl.ds(part * padded, padded), :],
                home_ref.at[:, :, pl.ds(part * LANES, LANES)],
                sems.at[1 + part],
            )
            for part in range(width // LANES)
        ],
    )
    other_previous = other_even_ref[...] + other_odd_ref[...]
    logits = dot_nt(anchors_ref[...], previous_ref[...]) + dot_nt(other_anchors_ref[...], other_previous)
    weights = jnp.exp(SCALE * logits - as_column(lse_ref[...])).astype(BF16)
    anchor_ref[...] = toward_ref[...] + SCALE * dot_nn(weights, previous_ref[...])
    for copy in copies:
        copy.wait()
    digits = packed_ref[...].astype(F32)
    asked = listed_row(blocks, per_peer, padded, digits[:, 2, :].astype(BF16), digits[:, 3, :].astype(BF16))
    put = one_hot(iota((rows, blocks * padded), 0) == asked)
    home = dot_nn(put, home_ref[...].reshape(blocks * padded, width))
    partner_ref[...] = SCALE * dot_tn(weights, anchors_ref[...]) - SCALE * home


def final_kernel(fetched_hbm, slot_hbm, anchor_hbm, out_ref, fetched_ref, slot_ref, anchor_ref, sems):
    rows, width = anchor_ref.shape
    copies = begin(
        (slot_hbm, slot_ref, sems.at[0]), (fetched_hbm, fetched_ref, sems.at[1]), (anchor_hbm, anchor_ref, sems.at[2])
    )
    copies[0].wait()
    slot = as_column(slot_ref[...].astype(F32)).astype(I32)
    pick = one_hot(iota((rows, rows), 1) == slot)
    copies[1].wait()
    copies[2].wait()
    out_ref[...] = anchor_ref[...] - SCALE * dot_nn(pick, fetched_ref[...])


def call(kernel, name, flops, outs, operands, spaces=None, out_space=None, scratch=(), aliases=None, limit=63_400_000):
    size = sum(value.size * value.dtype.itemsize for value in (*operands, *outs))
    spaces = spaces or "v" * len(operands)
    specs = [pl.BlockSpec(memory_space={"v": pltpu.VMEM, "h": pltpu.HBM}[space]) for space in spaces]
    return pl.pallas_call(
        kernel,
        out_shape=outs,
        name=name,
        in_specs=specs,
        out_specs=tuple(pl.BlockSpec(memory_space=space) for space in out_space or (pltpu.VMEM,) * len(outs)),
        scratch_shapes=list(scratch),
        input_output_aliases=aliases or {},
        cost_estimate=pl.CostEstimate(flops=flops, bytes_accessed=size, transcendentals=0),
        compiler_params=pltpu.CompilerParams(vmem_limit_bytes=limit),
    )(*operands)


def on_device(anchors, partners, row_lse, anchor_acc, partner_acc, match_dev, match_row):
    rows, width = anchors.shape
    blocks = lax.axis_size("blk")
    per_peer = rows // blocks
    shape = jax.ShapeDtypeStruct
    dma = pltpu.SemaphoreType.DMA
    cube = 2 * rows * rows * width

    assert per_peer <= LANES and width % LANES == 0
    padded = -(-per_peer // 16) * 16
    tall = width // LANES * padded + EXTRA

    send, slot = call(
        functools.partial(rank_kernel, blocks, per_peer, padded), "rank", COST["rank"] * cube // 4,
        (shape((blocks, tall, LANES), BF16), shape((1, rows), I32)),
        (match_dev, match_row, anchors), spaces="hhh", out_space=(pltpu.HBM, pltpu.VMEM),
        scratch=(
            pltpu.VMEM((rows,), I32), pltpu.VMEM((rows,), I32), pltpu.VMEM((rows, width), BF16),
            pltpu.VMEM((blocks, padded, width), BF16), pltpu.VMEM((blocks, EXTRA, LANES), F32),
            pltpu.VMEM((blocks, EXTRA, LANES), BF16), dma((4 + width // LANES,)),
        ),
    )
    got = lax.all_to_all(send, "blk", split_axis=0, concat_axis=0, tiled=True)

    other_anchors = shifted(anchors, "mp", 1)
    other_partners = shifted(partners, "mp", 1)
    got, ring_partners = lax.optimization_barrier((got, partners))
    previous = shifted(ring_partners, "blk", 1)
    got, other_anchors = lax.optimization_barrier((got, other_anchors))
    across = [(2 * block + half, 2 * block + 1 - half) for block in range(0, blocks, 2) for half in range(2)]
    other_even = lax.ppermute(previous, ("blk", "mp"), across)
    other_odd = lax.ppermute(other_partners, "blk", [(block, block + 1) for block in range(0, blocks, 2)])

    (found,) = call(
        functools.partial(serve_kernel, blocks, per_peer), "serve", COST["serve"] * cube // 4,
        (shape((rows, width), BF16),),
        (got, partners), spaces="hh", limit=SERVE,
        scratch=(pltpu.VMEM((blocks, EXTRA, LANES), BF16), pltpu.VMEM((rows, width), BF16), dma((2,))),
    )
    fetched = lax.all_to_all(
        found.reshape(blocks, per_peer, width), "blk", split_axis=0, concat_axis=0, tiled=True
    ).reshape(rows, width)

    lse_row = row_lse.reshape(1, rows)
    toward, staying = call(
        own_kernel, "own", COST["own"] * cube // 4,
        (shape((rows, width), F32), shape((rows, width), BF16)),
        (anchors, other_anchors, partners, other_partners, lse_row, anchor_acc, partner_acc), limit=MID,
    )
    arrived = shifted(staying, "blk", 1)
    anchor_part, partner_part = call(
        functools.partial(prior_kernel, blocks, per_peer, padded), "prior", COST["prior"] * cube // 4,
        (shape((rows, width), F32), shape((rows, width), F32)),
        (anchors, other_anchors, previous, other_even, other_odd, lse_row, toward, got), spaces="vvvvvvvh", limit=MID,
        scratch=(
            pltpu.VMEM((blocks, padded, width), BF16), pltpu.VMEM((blocks, EXTRA, LANES), BF16),
            dma((1 + width // LANES,)),
        ),
    )
    partner_out = arrived.astype(F32) + partner_part
    (anchor_grad,) = call(
        final_kernel, "final", COST["final"] * cube // 4,
        (shape((rows, width), F32),),
        (fetched, slot, anchor_part), spaces="hhh",
        scratch=(
            pltpu.VMEM((rows, width), BF16), pltpu.VMEM(slot.shape, I32), pltpu.VMEM((rows, width), F32), dma((3,)),
        ),
    )
    return anchor_grad, partner_out


def solution(mesh):
    return jax.shard_map(
        on_device,
        mesh=mesh,
        in_specs=(
            P("blk", "mp"),
            P("blk", "mp"),
            P("blk"),
            P("blk", "mp"),
            P("blk", "mp"),
            P("blk"),
            P("blk"),
        ),
        out_specs=(P("blk", "mp"), P("blk", "mp")),
        check_vma=False,
    )
```

```python
import functools
import jax
import jax.numpy as jnp
from jax import lax
from jax.experimental import pallas as pl
from jax.experimental.pallas import tpu as pltpu
from jax.sharding import PartitionSpec as P

SCALE = 10.0
LANES = 128
EXTRA = 8
COST = dict(rank=1, serve=0, own=16, prior=16, final=8)
MID = 40_000_000
SERVE = 63_400_000
BF16 = jnp.bfloat16
F32 = jnp.float32
I32 = jnp.int32


def shifted(value, axis, steps):
    count = lax.axis_size(axis)
    pairs = [(source, (source + steps) % count) for source in range(count)]
    return lax.ppermute(value, axis, pairs)


def dot_nt(left, right):
    return lax.dot_general(left, right, (((1,), (1,)), ((), ())), preferred_element_type=F32)


def dot_nn(left, right):
    return lax.dot_general(left, right, (((1,), (0,)), ((), ())), preferred_element_type=F32)


def dot_tn(left, right):
    return lax.dot_general(left, right, (((0,), (0,)), ((), ())), preferred_element_type=F32)


def iota(shape, dimension):
    return lax.broadcasted_iota(I32, shape, dimension)


def one_hot(condition):
    return jnp.where(condition, 1.0, 0.0).astype(BF16)


def split_digits(values):
    return (values >> 8).astype(F32), (values & 255).astype(F32)


def begin(*pairs):
    copies = [pltpu.make_async_copy(*pair) for pair in pairs]
    for copy in copies:
        copy.start()
    return copies


def rank_kernel(
    blocks, per_peer, padded, dev_hbm, row_hbm, anchors_hbm, send_hbm, slot_ref,
    dev_ref, row_ref, anchors_ref, ordered_ref, digits_ref, packed_ref, sems,
):
    copies = begin(
        (dev_hbm, dev_ref, sems.at[0]), (row_hbm, row_ref, sems.at[1]), (anchors_hbm, anchors_ref, sems.at[2])
    )
    rows, width = anchors_ref.shape
    earlier = one_hot(iota((rows, rows), 0) < iota((rows, rows), 1))
    digits_ref[...] = jnp.zeros_like(digits_ref)
    copies[0].wait()
    dev = dev_ref[...].reshape(1, rows)
    chosen = iota((blocks, rows), 0) == dev
    before = dot_nn(one_hot(chosen), earlier)
    rank = jnp.sum(jnp.where(chosen, before, 0.0), axis=0, keepdims=True).astype(I32)
    slot_ref[...] = dev * per_peer + rank
    after = jnp.where(dev == blocks - 1, 0, dev + 1)
    pick = one_hot(iota((blocks * padded, rows), 0) == after * padded + rank)
    copies[2].wait()
    ordered = dot_nn(pick, anchors_ref[...]).astype(BF16)
    ordered_ref[...] = ordered.reshape(ordered_ref.shape)
    outgoing = begin(*[
        (
            ordered_ref.at[:, :, pl.ds(part * LANES, LANES)],
            send_hbm.at[:, pl.ds(part * padded, padded), :],
            sems.at[3 + part],
        )
        for part in range(width // LANES)
    ])
    place = one_hot(iota((LANES, rows), 0) == rank)
    copies[1].wait()
    for digit, values in enumerate(split_digits(row_ref[...].reshape(1, rows))):
        wanted = dot_nt(jnp.where(chosen, values, 0.0).astype(BF16), place)
        digits_ref[:, digit, :] = wanted
        digits_ref[1:, 2 + digit, :] = wanted[:-1]
        digits_ref[:1, 2 + digit, :] = wanted[-1:]
    packed_ref[...] = digits_ref[...].astype(BF16)
    outgoing += begin((packed_ref, send_hbm.at[:, pl.ds(width // LANES * padded, EXTRA), :], sems.at[3 + width // LANES]))
    for copy in outgoing:
        copy.wait()


def listed_column(blocks, per_peer, high, low):
    count = blocks * per_peer
    spread = one_hot(iota((count, LANES), 1) == iota((count, LANES), 0) % per_peer)
    values = 256.0 * dot_nt(spread, high) + dot_nt(spread, low)
    mine = iota((count, blocks), 1) == iota((count, blocks), 0) // per_peer
    return jnp.sum(jnp.where(mine, values, 0.0), axis=1, keepdims=True).astype(I32)


def listed_row(blocks, per_peer, padded, high, low):
    count = blocks * padded
    place = iota((LANES, count), 1) % padded
    spread = one_hot(iota((LANES, count), 0) == place)
    values = 256.0 * dot_nn(high, spread) + dot_nn(low, spread)
    mine = iota((blocks, count), 0) == iota((blocks, count), 1) // padded
    asked = jnp.sum(jnp.where(mine, values, 0.0), axis=0, keepdims=True).astype(I32)
    return jnp.where(iota((1, count), 1) % padded < per_peer, asked, -1)


def serve_kernel(blocks, per_peer, got_hbm, partners_hbm, send_ref, packed_ref, partners_ref, sems):
    rows, width = partners_ref.shape
    table, fetch = begin(
        (got_hbm.at[:, pl.ds(got_hbm.shape[1] - EXTRA, EXTRA), :], packed_ref, sems.at[0]),
        (partners_hbm, partners_ref, sems.at[1]),
    )
    table.wait()
    digits = packed_ref[...].astype(F32)
    asked = listed_column(blocks, per_peer, digits[:, 0, :].astype(BF16), digits[:, 1, :].astype(BF16))
    pick = one_hot(asked == iota((rows, rows), 1))
    fetch.wait()
    send_ref[...] = dot_nn(pick, partners_ref[...]).astype(BF16)


def as_column(row):
    count = row.shape[1]
    diagonal = iota((count, count), 0) == iota((count, count), 1)
    return jnp.sum(jnp.where(diagonal, row, 0.0), axis=1, keepdims=True)


def own_kernel(
    anchors_ref, other_anchors_ref, partners_ref, other_partners_ref, lse_ref, anchor_acc_ref, partner_acc_ref,
    toward_ref, staying_ref,
):
    logits = dot_nt(anchors_ref[...], partners_ref[...]) + dot_nt(other_anchors_ref[...], other_partners_ref[...])
    weights = jnp.exp(SCALE * logits - as_column(lse_ref[...])).astype(BF16)
    staying = partner_acc_ref[...] + SCALE * dot_tn(weights, anchors_ref[...])
    staying_ref[...] = staying.astype(BF16)
    toward_ref[...] = anchor_acc_ref[...] + SCALE * dot_nn(weights, partners_ref[...])


def prior_kernel(
    blocks, per_peer, padded,
    anchors_ref, other_anchors_ref, previous_ref, other_even_ref, other_odd_ref, lse_ref, toward_ref, got_hbm,
    anchor_ref, partner_ref, home_ref, packed_ref, sems,
):
    rows, width = anchors_ref.shape
    copies = begin(
        (got_hbm.at[:, pl.ds(width // LANES * padded, EXTRA), :], packed_ref, sems.at[0]),
        *[
            (
                got_hbm.at[:, pl.ds(part * padded, padded), :],
                home_ref.at[:, :, pl.ds(part * LANES, LANES)],
                sems.at[1 + part],
            )
            for part in range(width // LANES)
        ],
    )
    other_previous = other_even_ref[...] + other_odd_ref[...]
    logits = dot_nt(anchors_ref[...], previous_ref[...]) + dot_nt(other_anchors_ref[...], other_previous)
    weights = jnp.exp(SCALE * logits - as_column(lse_ref[...])).astype(BF16)
    anchor_ref[...] = toward_ref[...] + SCALE * dot_nn(weights, previous_ref[...])
    for copy in copies:
        copy.wait()
    digits = packed_ref[...].astype(F32)
    asked = listed_row(blocks, per_peer, padded, digits[:, 2, :].astype(BF16), digits[:, 3, :].astype(BF16))
    put = one_hot(iota((rows, blocks * padded), 0) == asked)
    home = dot_nn(put, home_ref[...].reshape(blocks * padded, width))
    partner_ref[...] = SCALE * dot_tn(weights, anchors_ref[...]) - SCALE * home


def final_kernel(fetched_hbm, slot_hbm, anchor_hbm, out_ref, fetched_ref, slot_ref, anchor_ref, sems):
    rows, width = anchor_ref.shape
    copies = begin(
        (slot_hbm, slot_ref, sems.at[0]), (fetched_hbm, fetched_ref, sems.at[1]), (anchor_hbm, anchor_ref, sems.at[2])
    )
    copies[0].wait()
    slot = as_column(slot_ref[...].astype(F32)).astype(I32)
    pick = one_hot(iota((rows, rows), 1) == slot)
    copies[1].wait()
    copies[2].wait()
    out_ref[...] = anchor_ref[...] - SCALE * dot_nn(pick, fetched_ref[...])


def call(kernel, name, flops, outs, operands, spaces=None, out_space=None, scratch=(), aliases=None, limit=63_400_000):
    size = sum(value.size * value.dtype.itemsize for value in (*operands, *outs))
    spaces = spaces or "v" * len(operands)
    specs = [pl.BlockSpec(memory_space={"v": pltpu.VMEM, "h": pltpu.HBM}[space]) for space in spaces]
    return pl.pallas_call(
        kernel,
        out_shape=outs,
        name=name,
        in_specs=specs,
        out_specs=tuple(pl.BlockSpec(memory_space=space) for space in out_space or (pltpu.VMEM,) * len(outs)),
        scratch_shapes=list(scratch),
        input_output_aliases=aliases or {},
        cost_estimate=pl.CostEstimate(flops=flops, bytes_accessed=size, transcendentals=0),
        compiler_params=pltpu.CompilerParams(vmem_limit_bytes=limit),
    )(*operands)


def on_device(anchors, partners, row_lse, anchor_acc, partner_acc, match_dev, match_row):
    rows, width = anchors.shape
    blocks = lax.axis_size("blk")
    per_peer = rows // blocks
    shape = jax.ShapeDtypeStruct
    dma = pltpu.SemaphoreType.DMA
    cube = 2 * rows * rows * width

    assert per_peer <= LANES and width % LANES == 0
    padded = -(-per_peer // 16) * 16
    tall = width // LANES * padded + EXTRA

    send, slot = call(
        functools.partial(rank_kernel, blocks, per_peer, padded), "rank", COST["rank"] * cube // 4,
        (shape((blocks, tall, LANES), BF16), shape((1, rows), I32)),
        (match_dev, match_row, anchors), spaces="hhh", out_space=(pltpu.HBM, pltpu.VMEM),
        scratch=(
            pltpu.VMEM((rows,), I32), pltpu.VMEM((rows,), I32), pltpu.VMEM((rows, width), BF16),
            pltpu.VMEM((blocks, padded, width), BF16), pltpu.VMEM((blocks, EXTRA, LANES), F32),
            pltpu.VMEM((blocks, EXTRA, LANES), BF16), dma((4 + width // LANES,)),
        ),
    )
    got = lax.all_to_all(send, "blk", split_axis=0, concat_axis=0, tiled=True)

    other_anchors = shifted(anchors, "mp", 1)
    other_partners = shifted(partners, "mp", 1)
    got, ring_partners = lax.optimization_barrier((got, partners))
    previous = shifted(ring_partners, "blk", 1)
    across = [(2 * block + half, 2 * block + 1 - half) for block in range(0, blocks, 2) for half in range(2)]
    other_even = lax.ppermute(previous, ("blk", "mp"), across)
    other_odd = lax.ppermute(other_partners, "blk", [(block, block + 1) for block in range(0, blocks, 2)])

    (found,) = call(
        functools.partial(serve_kernel, blocks, per_peer), "serve", COST["serve"] * cube // 4,
        (shape((rows, width), BF16),),
        (got, partners), spaces="hh", limit=SERVE,
        scratch=(pltpu.VMEM((blocks, EXTRA, LANES), BF16), pltpu.VMEM((rows, width), BF16), dma((2,))),
    )
    found, other_anchors = lax.optimization_barrier((found, other_anchors))
    fetched = lax.all_to_all(
        found.reshape(blocks, per_peer, width), "blk", split_axis=0, concat_axis=0, tiled=True
    ).reshape(rows, width)

    lse_row = row_lse.reshape(1, rows)
    toward, staying = call(
        own_kernel, "own", COST["own"] * cube // 4,
        (shape((rows, width), F32), shape((rows, width), BF16)),
        (anchors, other_anchors, partners, other_partners, lse_row, anchor_acc, partner_acc), limit=MID,
    )
    arrived = shifted(staying, "blk", 1)
    anchor_part, partner_part = call(
        functools.partial(prior_kernel, blocks, per_peer, padded), "prior", COST["prior"] * cube // 4,
        (shape((rows, width), F32), shape((rows, width), F32)),
        (anchors, other_anchors, previous, other_even, other_odd, lse_row, toward, got), spaces="vvvvvvvh", limit=MID,
        scratch=(
            pltpu.VMEM((blocks, padded, width), BF16), pltpu.VMEM((blocks, EXTRA, LANES), BF16),
            dma((1 + width // LANES,)),
        ),
    )
    partner_out = arrived.astype(F32) + partner_part
    (anchor_grad,) = call(
        final_kernel, "final", COST["final"] * cube // 4,
        (shape((rows, width), F32),),
        (fetched, slot, anchor_part), spaces="hhh",
        scratch=(
            pltpu.VMEM((rows, width), BF16), pltpu.VMEM(slot.shape, I32), pltpu.VMEM((rows, width), F32), dma((3,)),
        ),
    )
    return anchor_grad, partner_out


def solution(mesh):
    return jax.shard_map(
        on_device,
        mesh=mesh,
        in_specs=(
            P("blk", "mp"),
            P("blk", "mp"),
            P("blk"),
            P("blk", "mp"),
            P("blk", "mp"),
            P("blk"),
            P("blk"),
        ),
        out_specs=(P("blk", "mp"), P("blk", "mp")),
        check_vma=False,
    )
```
